32 devices in a mesh: dom: 32 (over z, y, x, core).
Axes of the slice: x: 2, y: 2, z: 4, core: 2. Of those that a mesh axis runs over, the one named last changes fastest.
Arguments:
- grad_out: bfloat16 [16384, 256], P('dom'), may hold values from -6 to 6
- states: bfloat16 [16384, 256], P('dom'), may hold values from -0.98828125 to 0.98828125
- slopes: bfloat16 [16384, 256], P('dom'), may hold values from 0.099609375 to 1
- weight: bfloat16 [256, 256], replicated, may hold values from -0.375 to 0.375
- tiles: bfloat16 [768, 128, 128], P('dom'), may hold values from -0.23925781 to 0.23925781
- tile_dst: int32 [768], P('dom'), may hold values from 0 to 3, as said below
- tile_src: int32 [768], P('dom'), may hold values from 0 to 7, as said below
- tile_count: int32 [32], P('dom'), may hold values from 12 to 24, as said below
- send_rows: int32 [128, 128], P('dom'), may hold values from 0 to 511, as said below
Outputs:
- adjoint: float32 [16384, 256], P('dom')
- weight_grad: float32 [256, 256], replicated
The draws below stay inside these ranges and needn't reach their ends.
Inputs may be any that keep to these rules, and one draw needn't show every extreme that they name: `tile_src`: slot s of a partition with s < 4 has source tile 4 + s; slots 4 to 7 have destination and source tile s - 4; other used slots name a destination below 4 and a source below 8. `tile_dst`: destination tiles of a partition's slots. `tile_count`: some partition uses all 24 slots. `send_rows`: each list holds distinct local rows.
All inputs are finite; a program needn't handle non-finite values.
Results may differ from the reference program's by a relative error of at most 0.009.
Values may be sent and summed in bfloat16 or wider, within the bound.
No kernel may reach another device: no remote copies, remote signals or barrier semaphores. Data moves between devices by JAX's collectives and lax.ppermute only.
A program may use at most 64 MiB of HBM per device.

```python
import jax
import jax.numpy as jnp
from jax import lax

H = 256
TILE = 128
NB = 4
ITERS = 4
MAXT = 24
NODES = 16384
N_DOM = 32
DEVICES = 32


def draw_tile_dst(key, part):
    slot = jnp.arange(DEVICES * MAXT, dtype=jnp.int32) % MAXT
    random_dst = jax.random.randint(jax.random.fold_in(key, 11), (DEVICES * MAXT,), 0, NB, dtype=jnp.int32)
    return jnp.where(slot < 4, random_dst, jnp.where(slot < NB + 4, slot - 4, random_dst)).astype(jnp.int32)


def draw_tile_src(key, part):
    slot = jnp.arange(DEVICES * MAXT, dtype=jnp.int32) % MAXT
    random_src = jax.random.randint(jax.random.fold_in(key, 23), (DEVICES * MAXT,), 0, NB + 4, dtype=jnp.int32)
    return jnp.where(slot < 4, NB + slot, jnp.where(slot < NB + 4, slot - 4, random_src)).astype(jnp.int32)


def draw_tile_count(key, part):
    base = jax.random.randint(jax.random.fold_in(key, 5), (DEVICES,), MAXT // 2, MAXT + 1, dtype=jnp.int32)
    fullest = jax.random.randint(jax.random.fold_in(key, 7), (), 0, DEVICES, dtype=jnp.int32)
    lowest = (fullest + 1) % DEVICES
    position = jnp.arange(DEVICES, dtype=jnp.int32)
    counts = jnp.where(position == lowest, MAXT // 2, base)
    return jnp.where(position == fullest, MAXT, counts).astype(jnp.int32)


def draw_send_rows(key, part):
    keys = jax.random.split(jax.random.fold_in(key, 3), DEVICES * 4)
    return jax.vmap(lambda k: jax.random.permutation(k, NB * TILE)[:TILE])(keys).astype(jnp.int32)


def shard_levels(key, shape, pieces, least, largest):
    loudness = 1.0
    for dim, blocks in pieces:
        heights = jax.random.uniform(jax.random.fold_in(jax.random.fold_in(key, 6), dim), (blocks,), jnp.float32, least / len(pieces), largest / len(pieces))
        loudness = loudness * jnp.repeat(jnp.exp(heights), shape[dim] // blocks).reshape((-1,) + (1,) * (len(shape) - 1 - dim))
    return loudness


def normal_values(rng, extent, deviation, bound, shards=(), kind=jnp.bfloat16):
    entries = jax.random.normal(rng, extent, jnp.float32) * deviation
    if len(shards) > 0:
        entries = shard_levels(rng, extent, shards, -0.22, 0.18) * entries
    return jnp.clip(entries, min=-bound, max=bound).astype(kind)


def setup_inputs(seed: int = 0) -> dict:
    splits = jax.random.split(jax.random.key(seed), 10)
    grad_out = normal_values(splits[0], (NODES, H), 1.0, 6.0, ((0, 32),))
    states = jnp.clip(jax.random.uniform(splits[1], (NODES, H), jnp.float32, -0.98828125, 0.98828125) * shard_levels(splits[1], (NODES, H), ((0, 32),), -0.4, 0.0), -0.98828125, 0.98828125).astype(jnp.bfloat16)
    slopes = jnp.clip(0.099609375 + 0.9003906 * jax.random.uniform(splits[2], (NODES, H), jnp.float32) ** shard_levels(splits[2], (NODES, H), ((0, 32),), -0.2, 0.2), 0.099609375, 1.0).astype(jnp.bfloat16)
    weight = normal_values(splits[3], (H, H), H ** -0.5, 0.375)
    tiles = normal_values(splits[4], (MAXT * N_DOM, TILE, TILE), 0.04, 0.23925781, ((0, 32),))
    tile_dst = draw_tile_dst(jax.random.fold_in(splits[9], 71), 0)
    tile_src = draw_tile_src(jax.random.fold_in(splits[9], 71), 0)
    tile_count = draw_tile_count(jax.random.fold_in(splits[9], 71), 0)
    send_rows = draw_send_rows(jax.random.fold_in(splits[9], 71), 0)
    return {"grad_out": grad_out, "states": states, "slopes": slopes, "weight": weight, "tiles": tiles, "tile_dst": tile_dst, "tile_src": tile_src, "tile_count": tile_count, "send_rows": send_rows}


neighbour_steps = (1, -1, 16, -16)

def propagate_all(scaled, tiles, tile_dst, tile_src, tile_count, send_rows):
    parts = scaled.shape[0] // (NB * TILE)
    width = scaled.shape[1]
    field = scaled.reshape(parts, NB * TILE, width)
    lists = send_rows.reshape(parts, 4, TILE)
    sent = jax.vmap(lambda v, r: v[r])(field, lists)
    received = jnp.stack([jnp.roll(sent[:, n], neighbour_steps[n], axis=0) for n in range(4)], axis=1)
    extended = jnp.concatenate([field.reshape(parts, NB, TILE, width), received], axis=1)
    all_tiles = tiles.reshape(parts, MAXT, TILE, TILE)
    dsts = tile_dst.reshape(parts, MAXT)
    srcs = tile_src.reshape(parts, MAXT)

    def one_part(items):
        ext, tls, dst, src, count = items
        rows = ext[src].astype(jnp.float32)
        prod = jnp.einsum('tij,tjh->tih', tls.astype(jnp.float32), rows)
        used = (jnp.arange(MAXT) < count).astype(jnp.float32)
        prod = prod * used[:, None, None]
        total = jnp.zeros((NB, TILE, width), jnp.float32).at[dst].add(prod)
        return total.reshape(NB * TILE, width)
    out = lax.map(one_part, (extended, all_tiles, dsts, srcs, tile_count))
    return out.reshape(parts * NB * TILE, width)

def reference(grad_out, states, slopes, weight, tiles, tile_dst, tile_src, tile_count, send_rows):
    adjoint = grad_out.astype(jnp.float32)
    for step in range(ITERS):
        scaled = (slopes.astype(jnp.float32) * adjoint).astype(jnp.bfloat16)
        mixed = propagate_all(scaled, tiles, tile_dst, tile_src, tile_count, send_rows).astype(jnp.bfloat16)
        adjoint = grad_out.astype(jnp.float32) + lax.dot_general(mixed, weight, (((1,), (1,)), ((), ())), preferred_element_type=jnp.float32)
    final_scaled = (slopes.astype(jnp.float32) * adjoint).astype(jnp.bfloat16)
    final_mixed = propagate_all(final_scaled, tiles, tile_dst, tile_src, tile_count, send_rows)
    grad = lax.dot_general(states.astype(jnp.float32), final_mixed, (((0,), (0,)), ((), ())), precision=lax.Precision.HIGHEST)
    grad = grad / jnp.sqrt(jnp.float32(NODES))
    return (adjoint, grad)
```

```python
import functools

import jax
import jax.numpy as jnp
from jax import lax
from jax.experimental import pallas as pl
from jax.experimental.pallas import tpu as pltpu
from jax.sharding import PartitionSpec as P

ITERS = 4
REACH = 16
LISTS = 4
BF = jnp.bfloat16
F32 = jnp.float32
VMEM_BYTES = 24 * 1024 * 1024


def call(body, outs, ins, scratch=()):
    spaces = {"v": pltpu.VMEM, "s": pltpu.SMEM}
    return pl.pallas_call(
        body,
        out_shape=tuple(jax.ShapeDtypeStruct(shape, dtype) for shape, dtype in outs),
        in_specs=[pl.BlockSpec(memory_space=spaces[kind]) for kind in ins],
        out_specs=tuple(pl.BlockSpec(memory_space=pltpu.VMEM) for _ in outs),
        scratch_shapes=list(scratch),
        compiler_params=pltpu.CompilerParams(vmem_limit_bytes=VMEM_BYTES),
    )


def mm(a, b):
    return jnp.dot(a, b, preferred_element_type=F32)


def mm_rhs_t(a, b):
    return lax.dot_general(a, b, (((1,), (1,)), ((), ())), preferred_element_type=F32)


def mm_lhs_t(a, b):
    return lax.dot_general(a, b, (((0,), (0,)), ((), ())), preferred_element_type=F32)


def first_body(parity, lists, grad, slopes, scaled, pick, near, far, wide):
    size = lists.shape[1]
    rows = grad.shape[0]
    odd = parity[0] == 1
    order = (
        jnp.where(odd, lists[1:2, :], lists[0:1, :]),
        jnp.where(odd, lists[0:1, :], lists[1:2, :]),
        lists[2:3, :],
        lists[3:4, :],
    )
    column = lax.broadcasted_iota(jnp.int32, (size, rows), 1)
    for n in range(LISTS):
        wanted = jnp.broadcast_to(order[n], (size, size)).astype(F32).T.astype(jnp.int32)
        wanted = jnp.concatenate([wanted] * (rows // size), axis=1)
        pick[n * size : (n + 1) * size, :] = (wanted == column).astype(F32).astype(BF)
    value = (slopes[...].astype(F32) * grad[...].astype(F32)).astype(BF)
    scaled[...] = value
    sent = mm(pick[...], value).astype(BF)
    near[...] = sent[:size]
    far[...] = sent[size : 2 * size]
    wide[...] = sent[2 * size :]


def setup_body(
    parity, dst, src, count, tiles, pick, grad, slopes, scaled, states,
    own, edge, pick_own, pick_edge, pick_grad, pick_slopes, local, pick_local,
    back_own, back_near, back_far, back_wide, total,
):
    size = tiles.shape[1]
    blocks = total.shape[0]
    half = blocks // 2
    total[...] = jnp.zeros_like(total)
    even = parity[0] == 0

    def add(slot, carry):
        source = src[slot]
        swapped = even & ((source == half) | (source == half + 1))
        source = jnp.where(swapped, 2 * half + 1 - source, source)
        at = pl.ds(pl.multiple_of(dst[slot] * size, size), size)
        total[source, at, :] = total[source, at, :] + tiles[slot].astype(F32)
        return carry

    lax.fori_loop(0, count[0], add, 0)
    for b in range(half):
        at = slice(b * size, (b + 1) * size)
        own[:, at] = total[b].astype(BF)
        edge[:, at] = total[half + b].astype(BF)
    chosen = pick[...]
    pick_own[...] = mm(chosen, own[...]).astype(BF)
    pick_edge[...] = mm(chosen, edge[...]).astype(BF)
    pick_grad[...] = mm(chosen, grad[...]).astype(BF)
    pick_slopes[...] = mm(chosen, slopes[...]).astype(BF)
    local[...] = mm(own[...], scaled[...])
    pick_local[...] = mm(pick_own[...], scaled[...])
    back_own[...] = mm_lhs_t(own[...], states[...])
    back = mm_lhs_t(edge[...], states[...]).astype(BF)
    back_near[...] = back[:size]
    back_far[...] = back[size : 2 * size]
    back_wide[...] = back[2 * size :]


def send_body(near, far, wide, pick_local, pick_edge, pick_grad, pick_slopes, weight, near_out, far_out, wide_out):
    size = near.shape[0]
    came = jnp.concatenate([near[...], far[...], wide[...]], axis=0)
    mixed = (pick_local[...] + mm(pick_edge[...], came)).astype(BF)
    adjoint = pick_grad[...].astype(F32) + mm_rhs_t(mixed, weight[...])
    sent = (pick_slopes[...].astype(F32) * adjoint).astype(BF)
    near_out[...] = sent[:size]
    far_out[...] = sent[size : 2 * size]
    wide_out[...] = sent[2 * size :]


def own_body(near, far, wide, local, edge, grad, slopes, weight, own, pick_own, local_out, pick_local_out):
    came = jnp.concatenate([near[...], far[...], wide[...]], axis=0)
    mixed = (local[...] + mm(edge[...], came)).astype(BF)
    adjoint = grad[...].astype(F32) + mm_rhs_t(mixed, weight[...])
    scaled = (slopes[...].astype(F32) * adjoint).astype(BF)
    local_out[...] = mm(own[...], scaled)
    pick_local_out[...] = mm(pick_own[...], scaled)


def back_body(near, far, wide, back_own, pick, high, low):
    came = jnp.concatenate([near[...], far[...], wide[...]], axis=0)
    value = (back_own[...] + mm_lhs_t(pick[...], came)).T
    top = value.astype(BF)
    high[...] = top
    low[...] = (value - top.astype(F32)).astype(BF)


def last_body(factor, near, far, wide, local, edge, grad, slopes, weight, high, low, adjoint_out, partial):
    came = jnp.concatenate([near[...], far[...], wide[...]], axis=0)
    mixed = (local[...] + mm(edge[...], came)).astype(BF)
    adjoint = grad[...].astype(F32) + mm_rhs_t(mixed, weight[...])
    adjoint_out[...] = adjoint
    scaled = (slopes[...].astype(F32) * adjoint).astype(BF)
    partial[...] = (mm(high[...], scaled) + mm(low[...], scaled)) * factor


def exchange(near, far, wide, forward):
    count = lax.axis_size("dom")
    everyone = range(count)
    size = near.shape[0]
    ahead = [(p, (p + REACH) % count) for p in everyone]
    behind = [(p, (p - REACH) % count) for p in everyone]
    if not forward:
        ahead, behind = behind, ahead
    if ahead == behind:
        wide = lax.ppermute(wide, "dom", ahead)
    else:
        wide = jnp.concatenate(
            [lax.ppermute(wide[:size], "dom", ahead), lax.ppermute(wide[size:], "dom", behind)], axis=0
        )
    far = lax.ppermute(far, "dom", [(p, (p + 1 if p % 2 else p - 1) % count) for p in everyone])
    near = lax.ppermute(near, "dom", [(p, p ^ 1) for p in everyone])
    return near, far, wide


def summed(partial, parity):
    count = lax.axis_size("dom")
    if count & (count - 1):
        return lax.psum(partial, "dom")
    total = partial + lax.ppermute(partial, "dom", [(p, p + 1) for p in range(0, count, 2)])
    step = 2
    while step < count:
        mine = total.astype(BF)
        total = mine.astype(F32) + lax.ppermute(
            mine, "dom", [(p, p ^ step) for p in range(1, count, 2)]
        ).astype(F32)
        step *= 2
    theirs = lax.ppermute(total, "dom", [(p, p - 1) for p in range(1, count, 2)])
    return jnp.where(parity == 1, total, theirs)


def per_device(grad_out, states, slopes, weight, tiles, tile_dst, tile_src, tile_count, send_rows):
    rows, width = grad_out.shape
    slots, size, _ = tiles.shape
    cut = LISTS * size
    blocks = rows // size + LISTS
    parity = (lax.axis_index("dom") % 2).astype(jnp.int32).reshape(1)
    message = [((size, width), BF), ((size, width), BF), ((2 * size, width), BF)]

    scaled, pick, near, far, wide = call(
        first_body, [((rows, width), BF), ((cut, rows), BF)] + message, "svvv"
    )(parity, send_rows, grad_out, slopes)
    came = exchange(near, far, wide, True)
    (
        own, edge, pick_own, pick_edge, pick_grad, pick_slopes, local, pick_local, back_own, *back
    ) = call(
        setup_body,
        [
            ((rows, rows), BF), ((rows, cut), BF), ((cut, rows), BF), ((cut, cut), BF),
            ((cut, width), BF), ((cut, width), BF), ((rows, width), F32), ((cut, width), F32),
            ((rows, width), F32),
        ] + message,
        "ssssvvvvvv",
        [pltpu.VMEM((blocks, rows, size), F32)],
    )(parity, tile_dst, tile_src, tile_count, tiles, pick, grad_out, slopes, scaled, states)
    back_came = exchange(*back, False)
    high, low = call(back_body, [((width, rows), BF), ((width, rows), BF)], "vvvvv")(*back_came, back_own, pick)

    for step in range(ITERS - 1):
        sent = call(send_body, message, "v" * 8)(*came, pick_local, pick_edge, pick_grad, pick_slopes, weight)
        local_next = call(own_body, [((rows, width), F32), ((cut, width), F32)], "v" * 10)(
            *came, local, edge, grad_out, slopes, weight, own, pick_own
        )
        came = exchange(*sent, True)
        local, pick_local = local_next
    factor = 1.0 / float(lax.axis_size("dom") * rows) ** 0.5
    adjoint, partial = call(
        functools.partial(last_body, factor), [((rows, width), F32), ((width, width), F32)], "v" * 10
    )(*came, local, edge, grad_out, slopes, weight, high, low)
    return adjoint, summed(partial, parity[0])


def solution(mesh):
    in_specs = (
        P("dom", None),
        P("dom", None),
        P("dom", None),
        P(),
        P("dom", None, None),
        P("dom"),
        P("dom"),
        P("dom"),
        P("dom", None),
    )
    out_specs = (P("dom", None), P())
    return jax.shard_map(
        per_device, mesh=mesh, in_specs=in_specs, out_specs=out_specs, check_vma=False
    )
```

```python
import functools

import jax
import jax.numpy as jnp
from jax import lax
from jax.experimental import pallas as pl
from jax.experimental.pallas import tpu as pltpu
from jax.sharding import PartitionSpec as P


ITERS = 4
REACH = 16
LISTS = 4
BF = jnp.bfloat16
F32 = jnp.float32
VMEM_BYTES = 8 * 1024 * 1024


def call(body, outs, ins, scratch=()):
    spaces = {"v": pltpu.VMEM, "s": pltpu.SMEM, "h": pltpu.HBM}
    return pl.pallas_call(
        body,
        out_shape=tuple(jax.ShapeDtypeStruct(shape, dtype) for shape, dtype in outs),
        in_specs=[pl.BlockSpec(memory_space=spaces[kind]) for kind in ins],
        out_specs=tuple(pl.BlockSpec(memory_space=pltpu.VMEM) for _ in outs),
        scratch_shapes=list(scratch),
        compiler_params=pltpu.CompilerParams(vmem_limit_bytes=VMEM_BYTES),
    )


def in_hbm(*arrays):
    return [pltpu.with_memory_space_constraint(a, pltpu.HBM) for a in arrays]


def mm(a, b):
    return jnp.dot(a, b, preferred_element_type=F32)


def mm_rhs_t(a, b):
    return lax.dot_general(a, b, (((1,), (1,)), ((), ())), preferred_element_type=F32)


def mm_lhs_t(a, b):
    return lax.dot_general(a, b, (((0,), (0,)), ((), ())), preferred_element_type=F32)


def parity():
    return lax.rem(lax.axis_index("dom"), 2)


def side():
    index = lax.axis_index("dom")
    bits = (lax.axis_size("dom") - 1).bit_length()
    result = index & 1
    for bit in range(1, bits):
        result = result ^ ((index >> bit) & 1)
    return result


def first_body(
    lists_in, grad_in, slopes_in, tiles_in, states_in, weight_in,
    near, far, wide, scaled, pick, grad, slopes, tiles, states, weight, lists, sems,
):
    pairs = (
        (lists_in, lists), (grad_in, grad), (slopes_in, slopes),
        (tiles_in, tiles), (states_in, states), (weight_in, weight),
    )
    copies = [pltpu.make_async_copy(source, held, sems.at[n]) for n, (source, held) in enumerate(pairs)]
    for copy in copies:
        copy.start()
    size = lists.shape[1]
    rows = grad.shape[0]
    odd = parity() == 1
    copies[0].wait()
    order = (
        jnp.where(odd, lists[1:2, :], lists[0:1, :]),
        jnp.where(odd, lists[0:1, :], lists[1:2, :]),
        lists[2:3, :],
        lists[3:4, :],
    )
    column = lax.broadcasted_iota(jnp.int32, (size, rows), 1)
    for n in range(LISTS):
        wanted = jnp.broadcast_to(order[n], (size, size)).astype(F32).T.astype(jnp.int32)
        wanted = jnp.concatenate([wanted] * (rows // size), axis=1)
        pick[n * size : (n + 1) * size, :] = (wanted == column).astype(F32).astype(BF)
    copies[1].wait()
    copies[2].wait()
    value = (slopes[...].astype(F32) * grad[...].astype(F32)).astype(BF)
    scaled[...] = value
    sent = mm(pick[...], value).astype(BF)
    near[...] = sent[:size]
    far[...] = sent[size : 2 * size]
    wide[...] = sent[2 * size :]
    for copy in copies[3:]:
        copy.wait()


def setup_body(
    dst_in, src_in, count, tiles, pick, grad, slopes, scaled, states,
    own, edge, pick_own, pick_edge, pick_grad, pick_slopes, local, pick_local,
    back_own, back_near, back_far, back_wide, total, dst, src, sems,
):
    pairs = ((dst_in, dst), (src_in, src))
    copies = [pltpu.make_async_copy(source, held, sems.at[n]) for n, (source, held) in enumerate(pairs)]
    for copy in copies:
        copy.start()
    size = tiles.shape[1]
    blocks = total.shape[0]
    half = blocks // 2
    even = parity() == 0
    total[...] = jnp.zeros_like(total)
    chosen = pick[...]
    pick_grad[...] = mm(chosen, grad[...]).astype(BF)
    pick_slopes[...] = mm(chosen, slopes[...]).astype(BF)
    for copy in copies:
        copy.wait()

    def add(slot, carry):
        source = src[slot]
        swapped = even & ((source == half) | (source == half + 1))
        source = jnp.where(swapped, 2 * half + 1 - source, source)
        at = pl.ds(pl.multiple_of(dst[slot] * size, size), size)
        total[source, at, :] = total[source, at, :] + tiles[slot].astype(F32)
        return carry

    lax.fori_loop(0, count[0], add, 0)
    for b in range(half):
        at = slice(b * size, (b + 1) * size)
        own[:, at] = total[b].astype(BF)
        edge[:, at] = total[half + b].astype(BF)
    pick_own[...] = mm(chosen, own[...]).astype(BF)
    pick_edge[...] = mm(chosen, edge[...]).astype(BF)
    local[...] = mm(own[...], scaled[...])
    pick_local[...] = mm(pick_own[...], scaled[...])
    back_own[...] = mm_lhs_t(own[...], states[...])
    back = mm_lhs_t(edge[...], states[...]).astype(BF)
    back_near[...] = back[:size]
    back_far[...] = back[size : 2 * size]
    back_wide[...] = back[2 * size :]


def arrived(near, far, wide):
    size = wide.shape[0] // 2
    return jnp.concatenate([near[:size, :], far[:size, :], wide[...]], axis=0)


def send_body(
    near, far, wide, pick_local, pick_edge, pick_grad, pick_slopes, weight, *rest
):
    near_out, far_out, wide_out = rest[-3:]
    size = wide.shape[0] // 2
    came = arrived(near, far, wide)
    mixed = (pick_local[...] + mm(pick_edge[...], came)).astype(BF)
    adjoint = pick_grad[...].astype(F32) + mm_rhs_t(mixed, weight[...])
    sent = (pick_slopes[...].astype(F32) * adjoint).astype(BF)
    near_out[:size, :] = sent[:size]
    far_out[:size, :] = sent[size : 2 * size]
    wide_out[...] = sent[2 * size :]
    if len(rest) > 3:
        near_out[size:, :] = rest[0][...]
        far_out[size:, :] = rest[1][...]


def newest(near, far, wide, local, edge, grad, weight):
    mixed = (local[...] + mm(edge[...], arrived(near, far, wide))).astype(BF)
    return grad[...].astype(F32) + mm_rhs_t(mixed, weight[...])


def own_body(near, far, wide, local, edge, grad, slopes, weight, own, pick_own, local_out, pick_local_out):
    scaled = (slopes[...].astype(F32) * newest(near, far, wide, local, edge, grad, weight)).astype(BF)
    local_out[...] = mm(own[...], scaled)
    pick_local_out[...] = mm(pick_own[...], scaled)


def back_body(near, far, wide, back_own, pick, high, low):
    size = wide.shape[0] // 2
    came = jnp.concatenate([near[size:, :], far[size:, :], wide[...]], axis=0)
    value = (back_own[...] + mm_lhs_t(pick[...], came)).T
    top = value.astype(BF)
    high[...] = top
    low[...] = (value - top.astype(F32)).astype(BF)


def last_body(factor, near, far, wide, local, edge, grad, slopes, weight, high, low, kept, given):
    scaled = (slopes[...].astype(F32) * newest(near, far, wide, local, edge, grad, weight)).astype(BF)
    rows = kept.shape[0]
    at = side()
    for half, out in ((at, kept), (1 - at, given)):
        lines = pl.ds(pl.multiple_of(half * rows, rows), rows)
        out[...] = (mm(high[lines, :], scaled) + mm(low[lines, :], scaled)) * factor


def adjoint_body(near, far, wide, local, edge, grad, weight, out):
    out[...] = newest(near, far, wide, local, edge, grad, weight)


def join_body(total, other, out):
    rows = total.shape[0]
    at = side()
    out[pl.ds(pl.multiple_of(at * rows, rows), rows), :] = total[...]
    out[pl.ds(pl.multiple_of((1 - at) * rows, rows), rows), :] = other[...]


def swap_wide(wide, forward=True):
    count = lax.axis_size("dom")
    ahead = [(p, (p + REACH) % count) for p in range(count)]
    behind = [(p, (p - REACH) % count) for p in range(count)]
    if not forward:
        ahead, behind = behind, ahead
    if ahead == behind:
        return lax.ppermute(wide, "dom", ahead)
    size = wide.shape[0] // 2
    return jnp.concatenate(
        [lax.ppermute(wide[:size], "dom", ahead), lax.ppermute(wide[size:], "dom", behind)], axis=0
    )


def exchange(near, far, wide):
    count = lax.axis_size("dom")
    wide = swap_wide(wide)
    far = lax.ppermute(far, "dom", [(p, (p + 1 if p % 2 else p - 1) % count) for p in range(count)])
    near = lax.ppermute(near, "dom", [(p, p ^ 1) for p in range(count)])
    return near, far, wide


def summed(kept, given):
    count = lax.axis_size("dom")
    rows, width = kept.shape
    beside = [(p, p ^ 1) for p in range(count)]
    total = kept + lax.ppermute(given, "dom", beside)
    step = 2
    while step < count:
        mine = total.astype(BF)
        theirs = lax.ppermute(mine, "dom", [(p, p ^ step ^ 1) for p in range(count)])
        total = mine.astype(F32) + theirs.astype(F32)
        step *= 2
    other = lax.ppermute(total, "dom", beside)
    return call(join_body, [((2 * rows, width), F32)], "vv")(total, other)[0]


def per_device(grad_out, states, slopes, weight, tiles, tile_dst, tile_src, tile_count, send_rows):
    rows, width = grad_out.shape
    slots, size, _ = tiles.shape
    cut = LISTS * size
    blocks = rows // size + LISTS
    field = (rows, width)
    message = [((size, width), BF), ((size, width), BF), ((2 * size, width), BF)]
    longer = [((2 * size, width), BF)] * 3

    near, far, wide, scaled, pick, grad_out, slopes, tiles, states, weight = call(
        first_body,
        message + [
            (field, BF), ((cut, rows), BF), (field, BF), (field, BF), (tiles.shape, BF), (field, BF),
            (weight.shape, BF),
        ],
        "hhhhhh",
        [pltpu.VMEM(send_rows.shape, jnp.int32), pltpu.SemaphoreType.DMA((6,))],
    )(*in_hbm(send_rows, grad_out, slopes, tiles, states, weight))
    came = exchange(near, far, wide)
    (
        own, edge, pick_own, pick_edge, pick_grad, pick_slopes, local, pick_local, back_own,
        back_near, back_far, back_wide,
    ) = call(
        setup_body,
        [
            ((rows, rows), BF), ((rows, cut), BF), ((cut, rows), BF), ((cut, cut), BF),
            ((cut, width), BF), ((cut, width), BF), (field, F32), ((cut, width), F32),
            (field, F32),
        ] + message,
        "hhsvvvvvv",
        [
            pltpu.VMEM((blocks, rows, size), F32), pltpu.SMEM((slots,), jnp.int32),
            pltpu.SMEM((slots,), jnp.int32), pltpu.SemaphoreType.DMA((2,)),
        ],
    )(*in_hbm(tile_dst, tile_src), tile_count, tiles, pick, grad_out, slopes, scaled, states)

    for step in range(ITERS - 1):
        extra = (back_near, back_far) if step == 0 else ()
        operands = (*came, pick_local, pick_edge, pick_grad, pick_slopes, weight, *extra)
        sent = call(send_body, longer if extra else message, "v" * len(operands))(*operands)
        following = exchange(*sent)
        if step == 0:
            back_wide = swap_wide(back_wide, False)
        local, pick_local = call(own_body, [(field, F32), ((cut, width), F32)], "v" * 10)(
            *came, local, edge, grad_out, slopes, weight, own, pick_own
        )
        came = following
        if step == 0:
            back_came = (came[0], came[1], back_wide)
    high, low = call(back_body, [((width, rows), BF), ((width, rows), BF)], "vvvvv")(*back_came, back_own, pick)
    factor = 1.0 / float(lax.axis_size("dom") * rows) ** 0.5
    half = ((width // 2, width), F32)
    kept, given = call(functools.partial(last_body, factor), [half, half], "v" * 10)(
        *came, local, edge, grad_out, slopes, weight, high, low
    )
    (adjoint,) = call(adjoint_body, [(field, F32)], "v" * 7)(*came, local, edge, grad_out, weight)
    return adjoint, summed(kept, given)


def solution(mesh):
    in_specs = (
        P("dom", None),
        P("dom", None),
        P("dom", None),
        P(),
        P("dom", None, None),
        P("dom"),
        P("dom"),
        P("dom"),
        P("dom", None),
    )
    out_specs = (P("dom", None), P())
    return jax.shard_map(per_device, mesh=mesh, in_specs=in_specs, out_specs=out_specs, check_vma=False)
```

```python
import functools

import jax
import jax.numpy as jnp
from jax import lax
from jax.experimental import pallas as pl
from jax.experimental.pallas import tpu as pltpu
from jax.sharding import PartitionSpec as P


ITERS = 4
REACH = 16
LISTS = 4
BF = jnp.bfloat16
F32 = jnp.float32
VMEM_BYTES = 8 * 1024 * 1024


def call(body, outs, ins, scratch=()):
    spaces = {"v": pltpu.VMEM, "s": pltpu.SMEM, "h": pltpu.HBM}
    return pl.pallas_call(
        body,
        out_shape=tuple(jax.ShapeDtypeStruct(shape, dtype) for shape, dtype in outs),
        in_specs=[pl.BlockSpec(memory_space=spaces[kind]) for kind in ins],
        out_specs=tuple(pl.BlockSpec(memory_space=pltpu.VMEM) for _ in outs),
        scratch_shapes=list(scratch),
        compiler_params=pltpu.CompilerParams(vmem_limit_bytes=VMEM_BYTES),
    )


def in_hbm(*arrays):
    return [pltpu.with_memory_space_constraint(a, pltpu.HBM) for a in arrays]


def mm(a, b):
    return jnp.dot(a, b, preferred_element_type=F32)


def mm_rhs_t(a, b):
    return lax.dot_general(a, b, (((1,), (1,)), ((), ())), preferred_element_type=F32)


def mm_lhs_t(a, b):
    return lax.dot_general(a, b, (((0,), (0,)), ((), ())), preferred_element_type=F32)


def parity():
    return lax.rem(lax.axis_index("dom"), 2)


def side():
    index = lax.axis_index("dom")
    bits = (lax.axis_size("dom") - 1).bit_length()
    result = index & 1
    for bit in range(1, bits):
        result = result ^ ((index >> bit) & 1)
    return result


def first_body(
    lists_in, grad_in, slopes_in, tiles_in, states_in, weight_in,
    near, far, wide, scaled, pick, grad, slopes, tiles, states, weight, lists, sems,
):
    pairs = (
        (lists_in, lists), (grad_in, grad), (slopes_in, slopes),
        (tiles_in, tiles), (states_in, states), (weight_in, weight),
    )
    copies = [pltpu.make_async_copy(source, held, sems.at[n]) for n, (source, held) in enumerate(pairs)]
    for copy in copies:
        copy.start()
    size = lists.shape[1]
    rows = grad.shape[0]
    odd = parity() == 1
    copies[0].wait()
    order = (
        jnp.where(odd, lists[1:2, :], lists[0:1, :]),
        jnp.where(odd, lists[0:1, :], lists[1:2, :]),
        lists[2:3, :],
        lists[3:4, :],
    )
    column = lax.broadcasted_iota(jnp.int32, (size, rows), 1)
    for n in range(LISTS):
        wanted = jnp.broadcast_to(order[n], (size, size)).astype(F32).T.astype(jnp.int32)
        wanted = jnp.concatenate([wanted] * (rows // size), axis=1)
        pick[n * size : (n + 1) * size, :] = (wanted == column).astype(F32).astype(BF)
    copies[1].wait()
    copies[2].wait()
    value = (slopes[...].astype(F32) * grad[...].astype(F32)).astype(BF)
    scaled[...] = value
    sent = mm(pick[...], value).astype(BF)
    near[...] = sent[:size]
    far[...] = sent[size : 2 * size]
    wide[...] = sent[2 * size :]
    for copy in copies[3:]:
        copy.wait()


def setup_body(
    dst_in, src_in, count, tiles, pick, grad, slopes, scaled, states,
    own, edge, pick_own, pick_edge, pick_grad, pick_slopes, local, pick_local,
    back_own, back_near, back_far, back_wide_a, back_wide_b, total, dst, src, sems,
):
    pairs = ((dst_in, dst), (src_in, src))
    copies = [pltpu.make_async_copy(source, held, sems.at[n]) for n, (source, held) in enumerate(pairs)]
    for copy in copies:
        copy.start()
    size = tiles.shape[1]
    blocks = total.shape[0]
    half = blocks // 2
    even = parity() == 0
    total[...] = jnp.zeros_like(total)
    chosen = pick[...]
    pick_grad[...] = mm(chosen, grad[...]).astype(BF)
    pick_slopes[...] = mm(chosen, slopes[...]).astype(BF)
    for copy in copies:
        copy.wait()

    def add(slot, carry):
        source = src[slot]
        swapped = even & ((source == half) | (source == half + 1))
        source = jnp.where(swapped, 2 * half + 1 - source, source)
        at = pl.ds(pl.multiple_of(dst[slot] * size, size), size)
        total[source, at, :] = total[source, at, :] + tiles[slot].astype(F32)
        return carry

    lax.fori_loop(0, count[0], add, 0)
    for b in range(half):
        at = slice(b * size, (b + 1) * size)
        own[:, at] = total[b].astype(BF)
        edge[:, at] = total[half + b].astype(BF)
    pick_own[...] = mm(chosen, own[...]).astype(BF)
    pick_edge[...] = mm(chosen, edge[...]).astype(BF)
    local[...] = mm(own[...], scaled[...])
    pick_local[...] = mm(pick_own[...], scaled[...])
    back_own[...] = mm_lhs_t(own[...], states[...])
    back = mm_lhs_t(edge[...], states[...]).astype(BF)
    back_near[...] = back[:size]
    back_far[...] = back[size : 2 * size]
    back_wide_a[...] = back[2 * size : 3 * size]
    back_wide_b[...] = back[3 * size :]


def arrived(near, far, wide):
    size = wide.shape[0] // 2
    return jnp.concatenate([near[:size, :], far[:size, :], wide[...]], axis=0)


def send_body(
    near, far, wide, pick_local, pick_edge, pick_grad, pick_slopes, weight, *rest
):
    near_out, far_out, wide_out = rest[-3:]
    size = wide.shape[0] // 2
    came = arrived(near, far, wide)
    mixed = (pick_local[...] + mm(pick_edge[...], came)).astype(BF)
    adjoint = pick_grad[...].astype(F32) + mm_rhs_t(mixed, weight[...])
    sent = (pick_slopes[...].astype(F32) * adjoint).astype(BF)
    near_out[:size, :] = sent[:size]
    far_out[:size, :] = sent[size : 2 * size]
    wide_out[...] = sent[2 * size :]
    if len(rest) > 3:
        near_out[size:, :] = rest[0][...]
        far_out[size:, :] = rest[1][...]


def newest(near, far, wide, local, edge, grad, weight):
    mixed = (local[...] + mm(edge[...], arrived(near, far, wide))).astype(BF)
    return grad[...].astype(F32) + mm_rhs_t(mixed, weight[...])


def own_body(near, far, wide, local, edge, grad, slopes, weight, *rest):
    scaled = (slopes[...].astype(F32) * newest(near, far, wide, local, edge, grad, weight)).astype(BF)
    matrices, outs = rest[: len(rest) // 2], rest[len(rest) // 2 :]
    for matrix, out in zip(matrices, outs):
        out[...] = mm(matrix[...], scaled)


def back_body(near, far, wide_a, wide_b, back_own, pick, high, low):
    size = wide_a.shape[0]
    came = jnp.concatenate([near[size:, :], far[size:, :], wide_a[...], wide_b[...]], axis=0)
    value = (back_own[...] + mm_lhs_t(pick[...], came)).T
    top = value.astype(BF)
    high[...] = top
    low[...] = (value - top.astype(F32)).astype(BF)


def last_body(factor, near, far, wide, local, edge, grad, slopes, weight, high, low, kept, given):
    scaled = (slopes[...].astype(F32) * newest(near, far, wide, local, edge, grad, weight)).astype(BF)
    rows = kept.shape[0]
    at = side()
    for half, out in ((at, kept), (1 - at, given)):
        lines = pl.ds(pl.multiple_of(half * rows, rows), rows)
        out[...] = (mm(high[lines, :], scaled) + mm(low[lines, :], scaled)) * factor


def adjoint_body(near, far, wide, local, edge, grad, weight, out):
    out[...] = newest(near, far, wide, local, edge, grad, weight)


def join_body(total, other, out):
    rows = total.shape[0]
    at = side()
    out[pl.ds(pl.multiple_of(at * rows, rows), rows), :] = total[...]
    out[pl.ds(pl.multiple_of((1 - at) * rows, rows), rows), :] = other[...]


def swap_wide(wide, forward=True):
    count = lax.axis_size("dom")
    ahead = [(p, (p + REACH) % count) for p in range(count)]
    behind = [(p, (p - REACH) % count) for p in range(count)]
    if not forward:
        ahead, behind = behind, ahead
    if ahead == behind:
        return lax.ppermute(wide, "dom", ahead)
    size = wide.shape[0] // 2
    return jnp.concatenate(
        [lax.ppermute(wide[:size], "dom", ahead), lax.ppermute(wide[size:], "dom", behind)], axis=0
    )


def swap_list(rows, step):
    count = lax.axis_size("dom")
    return lax.ppermute(rows, "dom", [(p, (p + step) % count) for p in range(count)])


def exchange(near, far, wide):
    count = lax.axis_size("dom")
    wide = swap_wide(wide)
    far = lax.ppermute(far, "dom", [(p, (p + 1 if p % 2 else p - 1) % count) for p in range(count)])
    near = lax.ppermute(near, "dom", [(p, p ^ 1) for p in range(count)])
    return near, far, wide


def summed(kept, given):
    count = lax.axis_size("dom")
    rows, width = kept.shape
    beside = [(p, p ^ 1) for p in range(count)]
    total = kept + lax.ppermute(given, "dom", beside)
    step = 2
    while step < count:
        mine = total.astype(BF)
        theirs = lax.ppermute(mine, "dom", [(p, p ^ step ^ 1) for p in range(count)])
        total = mine.astype(F32) + theirs.astype(F32)
        step *= 2
    other = lax.ppermute(total, "dom", beside)
    return call(join_body, [((2 * rows, width), F32)], "vv")(total, other)[0]


def per_device(grad_out, states, slopes, weight, tiles, tile_dst, tile_src, tile_count, send_rows):
    rows, width = grad_out.shape
    slots, size, _ = tiles.shape
    cut = LISTS * size
    blocks = rows // size + LISTS
    field = (rows, width)
    message = [((size, width), BF), ((size, width), BF), ((2 * size, width), BF)]
    longer = [((2 * size, width), BF)] * 3

    near, far, wide, scaled, pick, grad_out, slopes, tiles, states, weight = call(
        first_body,
        message + [
            (field, BF), ((cut, rows), BF), (field, BF), (field, BF), (tiles.shape, BF), (field, BF),
            (weight.shape, BF),
        ],
        "hhhhhh",
        [pltpu.VMEM(send_rows.shape, jnp.int32), pltpu.SemaphoreType.DMA((6,))],
    )(*in_hbm(send_rows, grad_out, slopes, tiles, states, weight))
    came = exchange(near, far, wide)
    (
        own, edge, pick_own, pick_edge, pick_grad, pick_slopes, local, pick_local, back_own,
        back_near, back_far, back_wide_a, back_wide_b,
    ) = call(
        setup_body,
        [
            ((rows, rows), BF), ((rows, cut), BF), ((cut, rows), BF), ((cut, cut), BF),
            ((cut, width), BF), ((cut, width), BF), (field, F32), ((cut, width), F32),
            (field, F32),
        ] + [((size, width), BF)] * LISTS,
        "hhsvvvvvv",
        [
            pltpu.VMEM((blocks, rows, size), F32), pltpu.SMEM((slots,), jnp.int32),
            pltpu.SMEM((slots,), jnp.int32), pltpu.SemaphoreType.DMA((2,)),
        ],
    )(*in_hbm(tile_dst, tile_src), tile_count, tiles, pick, grad_out, slopes, scaled, states)

    back_wide_a = swap_list(back_wide_a, -REACH)
    back_wide_b = swap_list(back_wide_b, REACH)
    pick_local = (pick_local,)
    for step in range(ITERS - 1):
        extra = (back_near, back_far) if step == 0 else ()
        operands = (*came, *pick_local, pick_edge, pick_grad, pick_slopes, weight, *extra)
        sent = call(send_body, longer if extra else message, "v" * len(operands))(*operands)
        following = exchange(*sent)
        matrices = (own, pick_own) if step < ITERS - 2 else (own,)
        local, *pick_local = call(own_body, [((m.shape[0], width), F32) for m in matrices], "v" * (8 + len(matrices)))(
            *came, local, edge, grad_out, slopes, weight, *matrices
        )
        came = following
        if step == 0:
            back_came = (came[0], came[1], back_wide_a, back_wide_b)
    high, low = call(back_body, [((width, rows), BF), ((width, rows), BF)], "v" * 6)(*back_came, back_own, pick)
    factor = 1.0 / float(lax.axis_size("dom") * rows) ** 0.5
    half = ((width // 2, width), F32)
    kept, given = call(functools.partial(last_body, factor), [half, half], "v" * 10)(
        *came, local, edge, grad_out, slopes, weight, high, low
    )
    (adjoint,) = call(adjoint_body, [(field, F32)], "v" * 7)(*came, local, edge, grad_out, weight)
    return adjoint, summed(kept, given)


def solution(mesh):
    in_specs = (
        P("dom", None),
        P("dom", None),
        P("dom", None),
        P(),
        P("dom", None, None),
        P("dom"),
        P("dom"),
        P("dom"),
        P("dom", None),
    )
    out_specs = (P("dom", None), P())
    return jax.shard_map(per_device, mesh=mesh, in_specs=in_specs, out_specs=out_specs, check_vma=False)
```

```python
import functools

import jax
import jax.numpy as jnp
from jax import lax
from jax.experimental import pallas as pl
from jax.experimental.pallas import tpu as pltpu
from jax.sharding import PartitionSpec as P


ITERS = 4
REACH = 16
LISTS = 4
BF = jnp.bfloat16
F32 = jnp.float32
VMEM_BYTES = 8 * 1024 * 1024


def call(body, outs, ins, scratch=(), out_space=pltpu.VMEM):
    spaces = {"v": pltpu.VMEM, "s": pltpu.SMEM, "h": pltpu.HBM}
    return pl.pallas_call(
        body,
        out_shape=tuple(jax.ShapeDtypeStruct(shape, dtype) for shape, dtype in outs),
        in_specs=[pl.BlockSpec(memory_space=spaces[kind]) for kind in ins],
        out_specs=tuple(pl.BlockSpec(memory_space=out_space) for _ in outs),
        scratch_shapes=list(scratch),
        compiler_params=pltpu.CompilerParams(vmem_limit_bytes=VMEM_BYTES),
    )


def in_hbm(*arrays):
    return [pltpu.with_memory_space_constraint(a, pltpu.HBM) for a in arrays]


def mm(a, b):
    return jnp.dot(a, b, preferred_element_type=F32)


def mm_rhs_t(a, b):
    return lax.dot_general(a, b, (((1,), (1,)), ((), ())), preferred_element_type=F32)


def mm_lhs_t(a, b):
    return lax.dot_general(a, b, (((0,), (0,)), ((), ())), preferred_element_type=F32)


def parity():
    return lax.rem(lax.axis_index("dom"), 2)


def side():
    index = lax.axis_index("dom")
    bits = (lax.axis_size("dom") - 1).bit_length()
    result = index & 1
    for bit in range(1, bits):
        result = result ^ ((index >> bit) & 1)
    return result


def first_body(
    lists_in, grad_in, slopes_in, tiles_in, states_in, weight_in,
    near, far, wide, scaled, pick, grad, slopes, tiles, states, weight, lists, sems,
):
    pairs = (
        (lists_in, lists), (grad_in, grad), (slopes_in, slopes),
        (tiles_in, tiles), (states_in, states), (weight_in, weight),
    )
    copies = [pltpu.make_async_copy(source, held, sems.at[n]) for n, (source, held) in enumerate(pairs)]
    for copy in copies:
        copy.start()
    size = lists.shape[1]
    rows = grad.shape[0]
    odd = parity() == 1
    copies[0].wait()
    order = (
        jnp.where(odd, lists[1:2, :], lists[0:1, :]),
        jnp.where(odd, lists[0:1, :], lists[1:2, :]),
        lists[2:3, :],
        lists[3:4, :],
    )
    column = lax.broadcasted_iota(jnp.int32, (size, rows), 1)
    for n in range(LISTS):
        wanted = jnp.broadcast_to(order[n], (size, size)).astype(F32).T.astype(jnp.int32)
        wanted = jnp.concatenate([wanted] * (rows // size), axis=1)
        pick[n * size : (n + 1) * size, :] = (wanted == column).astype(F32).astype(BF)
    copies[1].wait()
    copies[2].wait()
    value = (slopes[...].astype(F32) * grad[...].astype(F32)).astype(BF)
    scaled[...] = value
    sent = mm(pick[...], value).astype(BF)
    near[...] = sent[:size]
    far[...] = sent[size : 2 * size]
    wide[...] = sent[2 * size :]
    for copy in copies[3:]:
        copy.wait()


def setup_body(
    dst_in, src_in, count, tiles, pick, grad, slopes, scaled, states,
    own, edge, pick_own, pick_edge, pick_grad, pick_slopes, local, pick_local,
    back_own, back_near, back_far, back_wide_a, back_wide_b, total, dst, src, sems,
):
    pairs = ((dst_in, dst), (src_in, src))
    copies = [pltpu.make_async_copy(source, held, sems.at[n]) for n, (source, held) in enumerate(pairs)]
    for copy in copies:
        copy.start()
    size = tiles.shape[1]
    blocks = total.shape[0]
    half = blocks // 2
    even = parity() == 0
    total[...] = jnp.zeros_like(total)
    chosen = pick[...]
    pick_grad[...] = mm(chosen, grad[...]).astype(BF)
    pick_slopes[...] = mm(chosen, slopes[...]).astype(BF)
    for copy in copies:
        copy.wait()

    def add(slot, carry):
        source = src[slot]
        swapped = even & ((source == half) | (source == half + 1))
        source = jnp.where(swapped, 2 * half + 1 - source, source)
        at = pl.ds(pl.multiple_of(dst[slot] * size, size), size)
        total[source, at, :] = total[source, at, :] + tiles[slot].astype(F32)
        return carry

    lax.fori_loop(0, count[0], add, 0)
    for b in range(half):
        at = slice(b * size, (b + 1) * size)
        own[:, at] = total[b].astype(BF)
        edge[:, at] = total[half + b].astype(BF)
    pick_own[...] = mm(chosen, own[...]).astype(BF)
    pick_edge[...] = mm(chosen, edge[...]).astype(BF)
    local[...] = mm(own[...], scaled[...])
    pick_local[...] = mm(pick_own[...], scaled[...])
    back_own[...] = mm_lhs_t(own[...], states[...])
    back = mm_lhs_t(edge[...], states[...]).astype(BF)
    back_near[...] = back[:size]
    back_far[...] = back[size : 2 * size]
    back_wide_a[...] = back[2 * size : 3 * size]
    back_wide_b[...] = back[3 * size :]


def arrived(near, far, wide):
    size = wide.shape[0] // 2
    return jnp.concatenate([near[:size, :], far[:size, :], wide[...]], axis=0)


def send_body(
    near, far, wide, pick_local, pick_edge, pick_grad, pick_slopes, weight, *rest
):
    near_out, far_out, wide_out = rest[-3:]
    size = wide.shape[0] // 2
    came = arrived(near, far, wide)
    mixed = (pick_local[...] + mm(pick_edge[...], came)).astype(BF)
    adjoint = pick_grad[...].astype(F32) + mm_rhs_t(mixed, weight[...])
    sent = (pick_slopes[...].astype(F32) * adjoint).astype(BF)
    near_out[:size, :] = sent[:size]
    far_out[:size, :] = sent[size : 2 * size]
    wide_out[...] = sent[2 * size :]
    if len(rest) > 3:
        near_out[size:, :] = rest[0][...]
        far_out[size:, :] = rest[1][...]


def newest(near, far, wide, local, edge, grad, weight):
    mixed = (local[...] + mm(edge[...], arrived(near, far, wide))).astype(BF)
    return grad[...].astype(F32) + mm_rhs_t(mixed, weight[...])


def own_body(near, far, wide, local, edge, grad, slopes, weight, *rest):
    scaled = (slopes[...].astype(F32) * newest(near, far, wide, local, edge, grad, weight)).astype(BF)
    matrices, outs = rest[: len(rest) // 2], rest[len(rest) // 2 :]
    for matrix, out in zip(matrices, outs):
        out[...] = mm(matrix[...], scaled)


def back_body(near, far, wide_a, wide_b, back_own, pick, high, low):
    size = wide_a.shape[0]
    came = jnp.concatenate([near[size:, :], far[size:, :], wide_a[...], wide_b[...]], axis=0)
    value = (back_own[...] + mm_lhs_t(pick[...], came)).T
    top = value.astype(BF)
    high[...] = top
    low[...] = (value - top.astype(F32)).astype(BF)


def last_body(factor, near, far, wide, local, edge, grad, slopes, weight, high, low, kept, given):
    scaled = (slopes[...].astype(F32) * newest(near, far, wide, local, edge, grad, weight)).astype(BF)
    rows = kept.shape[0]
    at = side()
    for half, out in ((at, kept), (1 - at, given)):
        lines = pl.ds(pl.multiple_of(half * rows, rows), rows)
        out[...] = (mm(high[lines, :], scaled) + mm(low[lines, :], scaled)) * factor


def adjoint_body(near, far, wide, local, edge, grad, weight, out):
    out[...] = newest(near, far, wide, local, edge, grad, weight)


def join_body(total, other, out, sems):
    rows = total.shape[0]
    at = side()
    copies = [
        pltpu.make_async_copy(held, out.at[pl.ds(pl.multiple_of(half * rows, rows), rows), :], sems.at[n])
        for n, (half, held) in enumerate(((at, total), (1 - at, other)))
    ]
    for copy in copies:
        copy.start()
    for copy in copies:
        copy.wait()


def swap_wide(wide, forward=True):
    count = lax.axis_size("dom")
    ahead = [(p, (p + REACH) % count) for p in range(count)]
    behind = [(p, (p - REACH) % count) for p in range(count)]
    if not forward:
        ahead, behind = behind, ahead
    if ahead == behind:
        return lax.ppermute(wide, "dom", ahead)
    size = wide.shape[0] // 2
    return jnp.concatenate(
        [lax.ppermute(wide[:size], "dom", ahead), lax.ppermute(wide[size:], "dom", behind)], axis=0
    )


def swap_list(rows, step):
    count = lax.axis_size("dom")
    return lax.ppermute(rows, "dom", [(p, (p + step) % count) for p in range(count)])


def exchange(near, far, wide):
    count = lax.axis_size("dom")
    wide = swap_wide(wide)
    far = lax.ppermute(far, "dom", [(p, (p + 1 if p % 2 else p - 1) % count) for p in range(count)])
    near = lax.ppermute(near, "dom", [(p, p ^ 1) for p in range(count)])
    return near, far, wide


def summed(kept, given):
    count = lax.axis_size("dom")
    rows, width = kept.shape
    beside = [(p, p ^ 1) for p in range(count)]
    total = kept + lax.ppermute(given, "dom", beside)
    for step in [1 << b for b in range(count.bit_length() - 2, 0, -1)]:
        mine = total.astype(BF)
        pairs = [(p, p ^ step ^ 1) for p in range(count)]
        parts = 2 if 2 * step == count else 1
        theirs = []
        for n in range(parts):
            theirs.append(lax.ppermute(mine[n * rows // parts : (n + 1) * rows // parts], "dom", pairs))
        total = mine.astype(F32) + jnp.concatenate(theirs, axis=0).astype(F32)
    other = lax.ppermute(total, "dom", beside)
    return call(
        join_body, [((2 * rows, width), F32)], "vv", [pltpu.SemaphoreType.DMA((2,))], pltpu.HBM
    )(total, other)[0]


def per_device(grad_out, states, slopes, weight, tiles, tile_dst, tile_src, tile_count, send_rows):
    rows, width = grad_out.shape
    slots, size, _ = tiles.shape
    cut = LISTS * size
    blocks = rows // size + LISTS
    field = (rows, width)
    message = [((size, width), BF), ((size, width), BF), ((2 * size, width), BF)]
    longer = [((2 * size, width), BF)] * 3

    near, far, wide, scaled, pick, grad_out, slopes, tiles, states, weight = call(
        first_body,
        message + [
            (field, BF), ((cut, rows), BF), (field, BF), (field, BF), (tiles.shape, BF), (field, BF),
            (weight.shape, BF),
        ],
        "hhhhhh",
        [pltpu.VMEM(send_rows.shape, jnp.int32), pltpu.SemaphoreType.DMA((6,))],
    )(*in_hbm(send_rows, grad_out, slopes, tiles, states, weight))
    came = exchange(near, far, wide)
    (
        own, edge, pick_own, pick_edge, pick_grad, pick_slopes, local, pick_local, back_own,
        back_near, back_far, back_wide_a, back_wide_b,
    ) = call(
        setup_body,
        [
            ((rows, rows), BF), ((rows, cut), BF), ((cut, rows), BF), ((cut, cut), BF),
            ((cut, width), BF), ((cut, width), BF), (field, F32), ((cut, width), F32),
            (field, F32),
        ] + [((size, width), BF)] * LISTS,
        "hhsvvvvvv",
        [
            pltpu.VMEM((blocks, rows, size), F32), pltpu.SMEM((slots,), jnp.int32),
            pltpu.SMEM((slots,), jnp.int32), pltpu.SemaphoreType.DMA((2,)),
        ],
    )(*in_hbm(tile_dst, tile_src), tile_count, tiles, pick, grad_out, slopes, scaled, states)

    back_wide_a = swap_list(back_wide_a, -REACH)
    back_wide_b = swap_list(back_wide_b, REACH)
    pick_local = (pick_local,)
    for step in range(ITERS - 1):
        extra = (back_near, back_far) if step == 0 else ()
        operands = (*came, *pick_local, pick_edge, pick_grad, pick_slopes, weight, *extra)
        sent = call(send_body, longer if extra else message, "v" * len(operands))(*operands)
        following = exchange(*sent)
        matrices = (own, pick_own) if step < ITERS - 2 else (own,)
        local, *pick_local = call(own_body, [((m.shape[0], width), F32) for m in matrices], "v" * (8 + len(matrices)))(
            *came, local, edge, grad_out, slopes, weight, *matrices
        )
        came = following
        if step == 0:
            back_came = (came[0], came[1], back_wide_a, back_wide_b)
    high, low = call(back_body, [((width, rows), BF), ((width, rows), BF)], "v" * 6)(*back_came, back_own, pick)
    factor = 1.0 / float(lax.axis_size("dom") * rows) ** 0.5
    half = ((width // 2, width), F32)
    kept, given = call(functools.partial(last_body, factor), [half, half], "v" * 10)(
        *came, local, edge, grad_out, slopes, weight, high, low
    )
    (adjoint,) = call(adjoint_body, [(field, F32)], "v" * 7)(*came, local, edge, grad_out, weight)
    return adjoint, summed(kept, given)


def solution(mesh):
    in_specs = (
        P("dom", None),
        P("dom", None),
        P("dom", None),
        P(),
        P("dom", None, None),
        P("dom"),
        P("dom"),
        P("dom"),
        P("dom", None),
    )
    out_specs = (P("dom", None), P())
    return jax.shard_map(per_device, mesh=mesh, in_specs=in_specs, out_specs=out_specs, check_vma=False)
```
